512 devices in a mesh: dp: 64 (over y, z_hi, x, core), fsdp: 8 (over z_lo).
Axes of the slice: x: 4, y: 4, z: 16 (z_hi: 2, z_lo: 8; z = z_hi * 8 + z_lo), core: 2. Of those that a mesh axis runs over, the one named last changes fastest.
Arguments:
- inputs: bfloat16 [65536, 4096], P(('dp', 'fsdp')), may hold values from -6 to 6
- out_grad: bfloat16 [65536, 2048], P(('dp', 'fsdp')), may hold values from -24 to 24
- weight: bfloat16 [4096, 2048], P('fsdp'), may hold values from -0.125 to 0.125
- proj_basis: bfloat16 [4096, 256], P('fsdp'), may hold values from -0.09375 to 0.09375
- first_moment: float32 [64, 8192], P('dp'), may hold values from -6 to 6
- second_moment: float32 [64, 8192], P('dp'), may hold values from 0.25 to 4
Outputs:
- input_grad: bfloat16 [65536, 4096], P(('dp', 'fsdp'))
- new_first: float32 [64, 8192], P('dp')
- new_second: float32 [64, 8192], P('dp')
- update: float32 [4096, 2048], P('fsdp', 'dp')
The draws below stay inside these ranges and needn't reach their ends.
All inputs are finite; a program needn't handle non-finite values.
Results may differ from the reference program's by a relative error of at most 0.0029.
Values may be sent and summed in bfloat16 or wider, within the bound.
No kernel may reach another device: no remote copies, remote signals or barrier semaphores. Data moves between devices by JAX's collectives and lax.ppermute only.
A program may use at most 64 MiB of HBM per device.

```python
import math
import jax
import jax.numpy as jnp
from jax import lax

D = 4096
F = 2048
RANK = 256
STEP = 1000
TOKENS = 65536
NBLK = 64
CBLK = 32


def raised(result, own_key, source, target, parts, factor):
    owner, partner = [(jnp.arange(result.shape[position]) // (result.shape[position] // parts)).reshape([-1 if axis == position else 1 for axis in range(result.ndim)]) for position in (source, target)]
    chosen = jax.random.permutation(own_key, parts)[partner]
    strong = (owner == chosen) | (owner == (partner + parts // 2) % parts)
    return jnp.where(strong, factor * result, result)


def level_of(stream_key, shape, split, smallest, high):
    def one(axis_at, parts):
        draws = jax.random.uniform(jax.random.fold_in(jax.random.fold_in(stream_key, 6), axis_at), (parts,), jnp.float32, smallest / len(split), high / len(split))
        return jnp.repeat(jnp.exp(draws), shape[axis_at] // parts).reshape((-1,) + (1,) * (len(shape) - axis_at - 1))

    level = one(*split[0])
    for cut in split[1:]:
        level = level * one(*cut)
    return level


def normal_values(rng, dims, scale, limit, split=(), dtype=jnp.bfloat16):
    result = jax.random.normal(rng, dims, jnp.float32) * scale
    if len(split) > 0:
        result = level_of(rng, dims, split, -0.22, 0.18) * result
    return jnp.clip(result, min=-limit, max=limit).astype(dtype)


def noise_with(stream_key, shape, width, limit, shards, heavy, dtype=jnp.bfloat16):
    drawn = width * jax.random.normal(stream_key, shape, jnp.float32)
    if shards:
        drawn = drawn * level_of(stream_key, shape, shards, -0.22, 0.18)
    return jnp.clip(raised(drawn, jax.random.fold_in(stream_key, 3), *heavy), -limit, limit).astype(dtype)


def setup_inputs(seed: int = 0) -> dict:
    splits = jax.random.split(jax.random.key(seed), 7)
    return {
        "inputs": normal_values(splits[0], (TOKENS, D), 1.0, 6.0, ((0, 512),)),
        "out_grad": noise_with(splits[1], (TOKENS, F), 1.0, 24.0, ((0, 512),), (0, 1, 512, 6.0)),
        "weight": normal_values(splits[2], (D, F), F ** -0.5, 0.125, ((0, 8),)),
        "proj_basis": normal_values(splits[3], (D, RANK), D ** -0.5, 0.09375, ((0, 8),)),
        "first_moment": normal_values(splits[4], (NBLK, RANK * CBLK), 1.0, 6.0, ((0, 64),), jnp.float32),
        "second_moment": jnp.clip(jnp.exp(math.log(4.0) - 2.7725887 * jax.random.uniform(splits[5], (NBLK, RANK * CBLK), jnp.float32) ** level_of(splits[5], (NBLK, RANK * CBLK), ((0, 64),), -0.2, 0.2)), 0.25, 4.0),
    }


beta_one = 0.9
beta_two = 0.999
epsilon = 1e-08

def reference(inputs, out_grad, weight, proj_basis, first_moment, second_moment):
    projected_in = jnp.dot(inputs, proj_basis, preferred_element_type=jnp.float32).astype(jnp.bfloat16)
    input_grad = lax.dot_general(out_grad, weight, (((1,), (1,)), ((), ())), preferred_element_type=jnp.float32).astype(jnp.bfloat16)
    low_rank = lax.dot_general(projected_in, out_grad, (((0,), (0,)), ((), ())), preferred_element_type=jnp.float32) * (1.0 / math.sqrt(TOKENS))
    blocked = low_rank.reshape(RANK, NBLK, CBLK).transpose(1, 0, 2).reshape(NBLK, RANK * CBLK)
    new_first = beta_one * first_moment + (1.0 - beta_one) * blocked
    new_second = beta_two * second_moment + (1.0 - beta_two) * blocked * blocked
    corr_one = 1.0 - beta_one ** STEP
    corr_two = 1.0 - beta_two ** STEP
    direction = (new_first / corr_one / (jnp.sqrt(new_second / corr_two) + epsilon)).astype(jnp.bfloat16)
    direction = direction.reshape(NBLK, RANK, CBLK).transpose(1, 0, 2).reshape(RANK, F)
    update = jnp.dot(proj_basis, direction, preferred_element_type=jnp.float32)
    return (input_grad, new_first, new_second, update)
```

```python
import math

import jax
import jax.numpy as jnp
from jax import lax
from jax.sharding import Mesh
from jax.sharding import PartitionSpec as P

STEP = 1000

beta_one = 0.9
beta_two = 0.999
epsilon = 1e-08

AXES = ("y", "zh", "x", "c", "q", "p")
SIZES = (4, 2, 4, 2, 4, 2)
PLANE = ("y", "x")
LINE = ("q", "p")
COLUMN = ("zh", "c", "q", "p")
SWAP = [(0, 1), (1, 0)]


def spread(block, axes, count):
    sent = jnp.broadcast_to(block[None], (count,) + block.shape)
    return lax.all_to_all(sent, axes, 0, 0, tiled=True)


def project_basis(proj_basis, plane, core):
    rows = proj_basis.shape[0] // 16
    half = proj_basis.shape[1] // 2
    piece = lax.dynamic_slice(proj_basis, (plane * rows, core * half), (rows, half))
    line = spread(piece, LINE, 8)
    whole = spread(line, PLANE, 16)
    return whole.transpose(1, 0, 2, 3).reshape(-1, half)


def weight_half(weight, plane, core):
    half = weight.shape[0] // 2
    rows = half // 16
    piece = lax.dynamic_slice(weight, (core * half + plane * rows, 0), (rows, weight.shape[1]))
    line = spread(piece, "q", 4)
    whole = spread(line, PLANE, 16)
    return whole.transpose(1, 0, 2, 3).reshape(4 * half, weight.shape[1])


def on_device(inputs, out_grad, weight, proj_basis, first_moment, second_moment):
    f32, bf16 = jnp.float32, jnp.bfloat16
    core = lax.axis_index("c")
    parity = lax.axis_index("p")
    plane = lax.axis_index(PLANE)
    tokens = inputs.shape[0] * 512
    scale_factor = 1.0 / math.sqrt(tokens)

    basis = project_basis(proj_basis, plane, core)
    grad_c = lax.ppermute(out_grad, "c", SWAP)
    inputs_c = lax.ppermute(inputs, "c", SWAP)
    wide = weight_half(weight, plane, core)
    grad_z = lax.ppermute(out_grad, "p", SWAP)
    grad_zc = lax.ppermute(grad_z, "c", SWAP)

    proj = jnp.concatenate(
        [
            jnp.dot(inputs, basis, preferred_element_type=f32).astype(bf16),
            jnp.dot(inputs_c, basis, preferred_element_type=f32).astype(bf16),
        ],
        axis=0,
    )
    chip_grad = jnp.concatenate([out_grad, grad_c], axis=0)
    low = (
        lax.dot_general(chip_grad, proj, (((0,), (0,)), ((), ())), preferred_element_type=f32)
        * scale_factor
    )
    half = low.shape[1]
    cols = low.shape[0] // 64
    low = low.reshape(4, 2, 4, 2 * cols, half).transpose(0, 2, 1, 3, 4).reshape(16, 4 * cols, half)
    low = lax.all_to_all(low, PLANE, 0, 0, tiled=True).sum(axis=0)
    low = low.reshape(2, 2, 1, cols, half).astype(bf16)
    low = jnp.broadcast_to(low, (2, 2, 8, cols, half)).reshape(32, cols, half)
    low = lax.all_to_all(low, COLUMN, 0, 0, tiled=True).reshape(2, 2, 8, cols, half)
    low = low.astype(f32).sum(axis=(0, 2))
    flat_grad = low.transpose(0, 2, 1).reshape(1, 2 * half * cols)

    new_first = beta_one * first_moment + (1.0 - beta_one) * flat_grad
    new_second = beta_two * second_moment + (1.0 - beta_two) * flat_grad * flat_grad
    corr_one = 1.0 - beta_one**STEP
    corr_two = 1.0 - beta_two**STEP
    direction = (new_first / corr_one / (jnp.sqrt(new_second / corr_two) + epsilon)).astype(bf16)
    direction = direction.reshape(2 * half, cols)
    update = jnp.dot(proj_basis, direction, preferred_element_type=f32)

    both = jnp.concatenate([grad_z, grad_zc, chip_grad], axis=0)
    feats = lax.dot_general(
        both, wide, (((1,), (1,)), ((), ())), preferred_element_type=f32
    ).astype(bf16)
    n = inputs.shape[0]
    back = lax.ppermute(feats[: 2 * n], "p", SWAP)
    mine = jnp.stack([feats[2 * n : 3 * n], back[:n]])
    theirs = jnp.stack([feats[3 * n :], back[n:]])
    other = lax.ppermute(theirs, "c", SWAP)
    mine, other = (v.reshape(2, n, 4, -1) for v in (mine, other))
    lower = jnp.where(core == 0, mine, other)
    upper = jnp.where(core == 0, other, mine)
    even = [jnp.where(parity == 0, v[0], v[1]) for v in (lower, upper)]
    odd = [jnp.where(parity == 0, v[1], v[0]) for v in (lower, upper)]
    input_grad = jnp.stack(even + odd, axis=2).reshape(n, -1)
    return (input_grad, new_first, new_second, update)


def solution(mesh):
    fine = Mesh(mesh.devices.reshape(SIZES), AXES)
    dp, fsdp = AXES[:4], AXES[4:]
    in_specs = (
        P(AXES, None),
        P(AXES, None),
        P(fsdp, None),
        P(fsdp, None),
        P(dp, None),
        P(dp, None),
    )
    out_specs = (P(AXES, None), P(dp, None), P(dp, None), P(fsdp, dp))
    return jax.shard_map(
        on_device, mesh=fine, in_specs=in_specs, out_specs=out_specs, check_vma=False
    )
```

```python
import functools
import math

import jax
import jax.numpy as jnp
from jax import lax
from jax.experimental import pallas as pl
from jax.experimental.pallas import tpu as pltpu
from jax.sharding import Mesh
from jax.sharding import PartitionSpec as P

STEP = 1000

beta_one = 0.9
beta_two = 0.999
epsilon = 1e-08

AXES = ("y", "zh", "x", "c", "q", "p")
SIZES = (4, 2, 4, 2, 4, 2)
PLANE = ("y", "x")
LINE = ("q", "p")
COLUMN = ("zh", "c", "q", "p")
SWAP = [(0, 1), (1, 0)]
F32, BF16 = jnp.float32, jnp.bfloat16
PARAMS = pltpu.CompilerParams(vmem_limit_bytes=40 * 1024 * 1024)


def spread(block, axes, count):
    sent = jnp.broadcast_to(block[None], (count,) + block.shape)
    return lax.all_to_all(sent, axes, 0, 0, tiled=True)


def dot(a, b, dims):
    return lax.dot_general(a, b, (dims, ((), ())), preferred_element_type=F32)


def low_kernel(scale, x0, x1, g0, g1, basis, out):
    shards, half = basis.shape[1], basis.shape[3]
    depth = basis.shape[0] * basis.shape[2]
    proj = []
    for x in (x0, x1):
        total = None
        for s in range(shards):
            part = dot(
                x[:, s * depth : (s + 1) * depth],
                basis[:, s].reshape(depth, half),
                ((1,), (0,)),
            )
            total = part if total is None else total + part
        proj.append(total.astype(BF16))
    width = out.shape[1] // 2
    for y in range(4):
        for zh in range(2):
            at = (y * 2 + zh) * 4 * width
            part = dot(g0[:, at : at + 4 * width], proj[0], ((0,), (0,))) + dot(
                g1[:, at : at + 4 * width], proj[1], ((0,), (0,))
            )
            part = part * scale
            for x in range(4):
                out[y * 4 + x, zh * width : (zh + 1) * width, :] = part[
                    x * width : (x + 1) * width
                ]


def low_rank(x0, x1, g0, g1, basis, scale):
    cols, half = g0.shape[1], basis.shape[3]
    n = x0.shape[0]
    flops = 4 * n * half * (x0.shape[1] + cols)
    return pl.pallas_call(
        functools.partial(low_kernel, scale),
        out_shape=jax.ShapeDtypeStruct((16, cols // 16, half), F32),
        compiler_params=PARAMS,
        cost_estimate=pl.CostEstimate(flops=flops, bytes_accessed=6 << 20, transcendentals=0),
        name="low_rank",
    )(x0, x1, g0, g1, basis)


def feature_kernel(core, a, b, own, rest, out):
    del core
    n = a.shape[0]

    def write(rows):
        out[:n, :] = dot(a[...], rows, ((1,), (1,))).astype(BF16)
        out[n:, :] = dot(b[...], rows, ((1,), (1,))).astype(BF16)

    @pl.when(pl.program_id(0) == 0)
    def _():
        write(own[...])

    @pl.when(pl.program_id(0) > 0)
    def _():
        write(rest[...].reshape(own.shape))


def features(core, a, b, own, rest):
    n, depth = a.shape
    feat = own.shape[0] // 2
    rows = rest.shape[2]
    spec = pltpu.PrefetchScalarGridSpec(
        num_scalar_prefetch=1,
        grid=(4,),
        in_specs=[
            pl.BlockSpec((n, depth), lambda r, c: (0, 0)),
            pl.BlockSpec((n, depth), lambda r, c: (0, 0)),
            pl.BlockSpec((feat, depth), lambda r, c: (c[0], 0)),
            pl.BlockSpec((16, None, rows, depth), lambda r, c: (0, jnp.maximum(r - 1, 0), 0, 0)),
        ],
        out_specs=pl.BlockSpec((2 * n, feat), lambda r, c: (0, r)),
    )
    return pl.pallas_call(
        feature_kernel,
        grid_spec=spec,
        out_shape=jax.ShapeDtypeStruct((2 * n, 4 * feat), BF16),
        compiler_params=PARAMS,
        cost_estimate=pl.CostEstimate(
            flops=16 * n * depth * feat, bytes_accessed=6 << 20, transcendentals=0
        ),
        name="features",
    )(core[None], a, b, own, rest)


def assemble_kernel(where, mine, core_own, core_back, back, out):
    quad, parity, core = where[0], where[1], where[2]
    feat = mine.shape[1] // 4
    for ref, par, half in (
        (mine, parity, core),
        (core_own, parity, 1 - core),
        (back, 1 - parity, core),
        (core_back, 1 - parity, 1 - core),
    ):
        for r in range(4):
            shard = lax.rem(quad + r, 4) * 2 + par
            at = pl.multiple_of((shard * 2 + half) * feat, feat)
            out[:, pl.ds(at, feat)] = ref[:, r * feat : (r + 1) * feat]


def assemble(where, mine, core_own, core_back, back):
    n, wide = core_own.shape
    spec = pltpu.PrefetchScalarGridSpec(
        num_scalar_prefetch=1,
        grid=(1,),
        in_specs=[pl.BlockSpec((n, wide), lambda i, w: (0, 0))] * 4,
        out_specs=pl.BlockSpec((n, 4 * wide), lambda i, w: (0, 0)),
    )
    return pl.pallas_call(
        assemble_kernel,
        grid_spec=spec,
        out_shape=jax.ShapeDtypeStruct((n, 4 * wide), BF16),
        compiler_params=PARAMS,
        cost_estimate=pl.CostEstimate(flops=0, bytes_accessed=2 << 20, transcendentals=0),
        name="assemble",
    )(where, mine, core_own, core_back, back)


def on_device(inputs, out_grad, weight, proj_basis, first_moment, second_moment):
    core = lax.axis_index("c")
    parity = lax.axis_index("p")
    quad = lax.axis_index("q")
    plane = lax.axis_index(PLANE)
    n, feat = inputs.shape[0], weight.shape[0] // 2
    scale = 1.0 / math.sqrt(n * 512)
    half = proj_basis.shape[1] // 2

    rows = feat // 16
    piece = lax.dynamic_slice(weight, (core * feat + plane * rows, 0), (rows, weight.shape[1]))
    p_rows = proj_basis.shape[0] // 16
    p_piece = lax.dynamic_slice(proj_basis, (plane * p_rows, core * half), (p_rows, half))
    line = jnp.stack(
        [lax.ppermute(piece, "q", [((i + r) % 4, i) for i in range(4)]) for r in (1, 2, 3)]
    )
    rest = lax.all_gather(line, PLANE, axis=0)
    p_line = spread(p_piece, LINE, 8)
    basis = spread(p_line, PLANE, 16)

    grad_z = lax.ppermute(out_grad, "p", SWAP)
    grad_c = lax.ppermute(out_grad, "c", SWAP)
    inputs_c = lax.ppermute(inputs, "c", SWAP)
    grad_zc = lax.ppermute(grad_z, "c", SWAP)
    basis, inputs_c, grad_c, grad_z, grad_zc = lax.optimization_barrier(
        (basis, inputs_c, grad_c, grad_z, grad_zc)
    )

    low = low_rank(inputs, inputs_c, out_grad, grad_c, basis, scale)
    cols = low.shape[1] // 4
    low = lax.all_to_all(low, PLANE, 0, 0, tiled=True).sum(axis=0)
    low = low.reshape(2, 2, 1, cols, half).astype(BF16)
    low = jnp.broadcast_to(low, (2, 2, 8, cols, half)).reshape(32, cols, half)
    low = lax.all_to_all(low, COLUMN, 0, 0, tiled=True).reshape(2, 2, 8, cols, half)
    low = low.astype(F32).sum(axis=(0, 2))
    flat_grad = low.transpose(0, 2, 1).reshape(1, 2 * half * cols)
    new_first = beta_one * first_moment + (1.0 - beta_one) * flat_grad
    new_second = beta_two * second_moment + (1.0 - beta_two) * flat_grad * flat_grad
    corr_one = 1.0 - beta_one**STEP
    corr_two = 1.0 - beta_two**STEP
    direction = (new_first / corr_one / (jnp.sqrt(new_second / corr_two) + epsilon)).astype(BF16)
    direction = direction.reshape(2 * half, cols)
    update = jnp.dot(proj_basis, direction, preferred_element_type=F32)

    far = features(core, grad_z, grad_zc, weight, rest)
    back = lax.ppermute(far, "p", SWAP)
    near = features(core, out_grad, grad_c, weight, rest)
    core_own = lax.ppermute(near[n:], "c", SWAP)
    core_back = lax.ppermute(back[n:], "c", SWAP)
    where = jnp.stack([quad, parity, core])
    input_grad = assemble(where, near, core_own, core_back, back)
    return (input_grad, new_first, new_second, update)


def solution(mesh):
    fine = Mesh(mesh.devices.reshape(SIZES), AXES)
    dp, fsdp = AXES[:4], AXES[4:]
    in_specs = (
        P(AXES, None),
        P(AXES, None),
        P(fsdp, None),
        P(fsdp, None),
        P(dp, None),
        P(dp, None),
    )
    out_specs = (P(AXES, None), P(dp, None), P(dp, None), P(fsdp, dp))
    return jax.shard_map(
        on_device, mesh=fine, in_specs=in_specs, out_specs=out_specs, check_vma=False
    )
```

```python
import functools
import math

import jax
import jax.numpy as jnp
from jax import lax
from jax.experimental import pallas as pl
from jax.experimental.pallas import tpu as pltpu
from jax.sharding import Mesh
from jax.sharding import PartitionSpec as P

STEP = 1000

beta_one = 0.9
beta_two = 0.999
epsilon = 1e-08

AXES = ("y", "zh", "x", "c", "q", "p")
SIZES = (4, 2, 4, 2, 4, 2)
PLANE = ("y", "x")
LINE = ("q", "p")
RING = ("zh", "q", "p")
COLUMN = ("zh", "c", "q", "p")
F32, BF16 = jnp.float32, jnp.bfloat16


def spread(block, axes, count):
    sent = jnp.broadcast_to(block[None], (count,) + block.shape)
    return lax.all_to_all(sent, axes, 0, 0, tiled=True)


def dot(a, b, dims):
    return lax.dot_general(a, b, (dims, ((), ())), preferred_element_type=F32)


def low_kernel(scale, x0, x1, g0, g1, basis, out):
    shards, half = 8, basis.shape[2]
    rows = basis.shape[1] // shards
    depth = 16 * rows
    proj = []
    for x in (x0, x1):
        total = None
        for s in range(shards):
            part = dot(
                x[:, s * depth : (s + 1) * depth],
                basis[:, s * rows : (s + 1) * rows, :].reshape(depth, half),
                ((1,), (0,)),
            )
            total = part if total is None else total + part
        proj.append(total.astype(BF16))
    width = out.shape[1] // 2
    for y in range(4):
        for zh in range(2):
            at = (y * 2 + zh) * 4 * width
            part = dot(g0[:, at : at + 4 * width], proj[0], ((0,), (0,))) + dot(
                g1[:, at : at + 4 * width], proj[1], ((0,), (0,))
            )
            part = part * scale
            for x in range(4):
                out[y * 4 + x, zh * width : (zh + 1) * width, :] = part[
                    x * width : (x + 1) * width
                ]


def low_rank(x0, x1, g0, g1, mixed, scale):
    n, cols = g0.shape
    half = mixed.shape[2]
    whole = lambda v: pl.BlockSpec(v.shape, lambda i: (0, 0))
    return pl.pallas_call(
        functools.partial(low_kernel, scale),
        grid=(1,),
        in_specs=[whole(x0), whole(x1), whole(g0), whole(g1)]
        + [pl.BlockSpec((16, 256, half), lambda i: (0, 0, 0))],
        out_specs=pl.BlockSpec((16, cols // 16, half), lambda i: (0, 0, 0)),
        out_shape=jax.ShapeDtypeStruct((16, cols // 16, half), F32),
        cost_estimate=pl.CostEstimate(
            flops=4 * n * half * (x0.shape[1] + cols), bytes_accessed=6 << 20, transcendentals=0
        ),
        name="low_rank",
    )(x0, x1, g0, g1, mixed)


def feature_kernel(pairs, core, *refs):
    del core
    tokens, (own, rest), outs = refs[: 2 * pairs], refs[2 * pairs : 2 * pairs + 2], refs[2 * pairs + 2 : -1]
    rows = refs[-1]
    n = tokens[0].shape[0]
    first = pl.program_id(0) == 0

    @pl.when(first)
    def _():
        rows[...] = own[...]

    @pl.when(jnp.logical_not(first))
    def _():
        for g in range(16):
            group = rest[:, g * 16 : (g + 1) * 16, :]
            rows[:, g * 128 : (g + 1) * 128] = group.reshape(rows.shape[0], 128)

    for i, out in enumerate(outs):
        for j in range(2):
            out[j * n : (j + 1) * n, :] = dot(tokens[2 * i + j][...], rows[...], ((1,), (1,))).astype(
                BF16
            )


def features(core, tokens, own, mixed):
    n, depth = tokens[0].shape
    feat = own.shape[0] // 2
    pairs = len(tokens) // 2
    spec = pltpu.PrefetchScalarGridSpec(
        num_scalar_prefetch=1,
        grid=(2,),
        in_specs=[pl.BlockSpec((n, depth), lambda r, c: (0, 0)) for _ in tokens]
        + [
            pl.BlockSpec((feat, depth), lambda r, c: (c[0], 0)),
            pl.BlockSpec((16, 256, 128), lambda r, c: (0, 1, 0)),
        ],
        out_specs=[pl.BlockSpec((2 * n, feat), lambda r, c: (0, r))] * pairs,
        scratch_shapes=[pltpu.VMEM((feat, depth), BF16)],
    )
    return pl.pallas_call(
        functools.partial(feature_kernel, pairs),
        grid_spec=spec,
        out_shape=[jax.ShapeDtypeStruct((2 * n, 2 * feat), BF16)] * pairs,
        cost_estimate=pl.CostEstimate(
            flops=1 << 20, bytes_accessed=1 << 16, transcendentals=0
        ),
        name="features",
    )(core[None], *tokens, own, mixed)


def assemble_kernel(where, near, up, down, down2, crossed, out):
    line, core = where[0], where[1]
    feat = near.shape[1] // 2
    for i, (ref, offset) in enumerate(((near, 0), (up, 1), (down, 7), (down2, 6))):
        for r in range(2):
            shard = lax.rem(line + offset + 4 * r, 8)
            at = pl.multiple_of((shard * 2 + core) * feat, feat)
            out[:, pl.ds(at, feat)] = ref[:, r * feat : (r + 1) * feat]
            at = pl.multiple_of((shard * 2 + 1 - core) * feat, feat)
            out[:, pl.ds(at, feat)] = crossed[i, :, r * feat : (r + 1) * feat]


def assemble(where, pieces, crossed):
    _, n, wide = crossed.shape
    spec = pltpu.PrefetchScalarGridSpec(
        num_scalar_prefetch=1,
        grid=(1,),
        in_specs=[pl.BlockSpec((n, wide), lambda i, w: (0, 0))] * 4
        + [pl.BlockSpec((4, n, wide), lambda i, w: (0, 0, 0))],
        out_specs=pl.BlockSpec((n, 8 * wide), lambda i, w: (0, 0)),
    )
    return pl.pallas_call(
        assemble_kernel,
        grid_spec=spec,
        out_shape=jax.ShapeDtypeStruct((n, 8 * wide), BF16),
        cost_estimate=pl.CostEstimate(flops=0, bytes_accessed=1 << 16, transcendentals=0),
        name="assemble",
    )(where, *pieces, crossed)


def ring(value, step):
    return lax.ppermute(value, RING, [(i, (i + step) % 16) for i in range(16)])


def swap_cores(value):
    return lax.ppermute(value, "c", [(0, 1), (1, 0)])


def on_device(inputs, out_grad, weight, proj_basis, first_moment, second_moment):
    core = lax.axis_index("c")
    line = lax.axis_index(LINE)
    plane = lax.axis_index(PLANE)
    n, feat = inputs.shape[0], weight.shape[0] // 2
    scale = 1.0 / math.sqrt(n * 512)
    half = proj_basis.shape[1] // 2

    rows = feat // 16
    piece = lax.dynamic_slice(weight, (core * feat + plane * rows, 0), (rows, weight.shape[1]))
    piece = lax.ppermute(piece, LINE, [(i, (i + 4) % 8) for i in range(8)])
    piece = piece.reshape(rows, 16, 128).transpose(1, 0, 2).reshape(256, 128)
    p_rows = proj_basis.shape[0] // 16
    p_piece = lax.dynamic_slice(proj_basis, (plane * p_rows, core * half), (p_rows, half))
    before = ring(out_grad, 1)
    after = ring(out_grad, -1)
    p_line = spread(p_piece, LINE, 8).reshape(256, half)
    p_line, before, after = lax.optimization_barrier((p_line, before, after))
    mixed = spread(jnp.concatenate([p_line, piece]), PLANE, 16)

    grad_c = swap_cores(out_grad)
    inputs_c = swap_cores(inputs)
    after2 = ring(after, -1)
    far = [before, swap_cores(before), after, swap_cores(after), after2, swap_cores(after2)]
    mixed, inputs_c, grad_c, far = lax.optimization_barrier((mixed, inputs_c, grad_c, far))

    low = low_rank(inputs, inputs_c, out_grad, grad_c, mixed, scale)
    cols = low.shape[1] // 4
    low = lax.all_to_all(low, PLANE, 0, 0, tiled=True).sum(axis=0)
    low = low.reshape(2, 2, 1, cols, half).astype(BF16)
    far_out = features(core, far, weight, mixed)
    (near,) = features(core, [out_grad, grad_c], weight, mixed)
    pieces = [near, ring(far_out[0], -1), ring(far_out[1], 1), ring(far_out[2], 2)]
    low, pieces = lax.optimization_barrier((low, pieces))
    low = jnp.broadcast_to(low, (2, 2, 8, cols, half)).reshape(32, cols, half)
    low = lax.all_to_all(low, COLUMN, 0, 0, tiled=True).reshape(2, 2, 8, cols, half)
    low = low.astype(F32).sum(axis=(0, 2))
    flat_grad = low.transpose(0, 2, 1).reshape(1, 2 * half * cols)
    new_first = beta_one * first_moment + (1.0 - beta_one) * flat_grad
    new_second = beta_two * second_moment + (1.0 - beta_two) * flat_grad * flat_grad
    corr_one = 1.0 - beta_one**STEP
    corr_two = 1.0 - beta_two**STEP
    direction = (new_first / corr_one / (jnp.sqrt(new_second / corr_two) + epsilon)).astype(BF16)
    direction = direction.reshape(2 * half, cols)
    update = jnp.dot(proj_basis, direction, preferred_element_type=F32)

    crossed = swap_cores(jnp.stack([v[n:] for v in pieces]))
    input_grad = assemble(jnp.stack([line, core]), pieces, crossed)
    return (input_grad, new_first, new_second, update)


def solution(mesh):
    fine = Mesh(mesh.devices.reshape(SIZES), AXES)
    dp, fsdp = AXES[:4], AXES[4:]
    in_specs = (
        P(AXES, None),
        P(AXES, None),
        P(fsdp, None),
        P(fsdp, None),
        P(dp, None),
        P(dp, None),
    )
    out_specs = (P(AXES, None), P(dp, None), P(dp, None), P(fsdp, dp))
    return jax.shard_map(
        on_device, mesh=fine, in_specs=in_specs, out_specs=out_specs, check_vma=False
    )
```

```python
import functools
import math

import jax
import jax.numpy as jnp
from jax import lax
from jax.experimental import pallas as pl
from jax.experimental.pallas import tpu as pltpu
from jax.sharding import Mesh
from jax.sharding import PartitionSpec as P

STEP = 1000

beta_one = 0.9
beta_two = 0.999
epsilon = 1e-08

AXES = ("y", "zh", "x", "c", "q", "p")
SIZES = (4, 2, 4, 2, 4, 2)
PLANE = ("y", "x")
LINE = ("q", "p")
RING = ("zh", "q", "p")
COLUMN = ("zh", "c", "q", "p")
F32, BF16 = jnp.float32, jnp.bfloat16
COST = 20 << 30
LINE_COST = 20 << 30
FEATURE_COST = 1 << 20
HBM = pl.BlockSpec(memory_space=pltpu.HBM)
VMEM = pl.BlockSpec(memory_space=pltpu.VMEM)
PARAMS = pltpu.CompilerParams(vmem_limit_bytes=20 * 1024 * 1024)


def spread(block, axes, count):
    sent = jnp.broadcast_to(block[None], (count,) + block.shape)
    return lax.all_to_all(sent, axes, 0, 0, tiled=True)


def dot(a, b, dims):
    return lax.dot_general(a, b, (dims, ((), ())), preferred_element_type=F32)


def low_kernel(scale, x0, x1, g0, g1, mixed, out, sent, sems):
    members, _, half = mixed.shape
    rows = 256 // 8
    depth = members * rows
    proj = []
    for x in (x0, x1):
        total = None
        for s in range(8):
            basis = mixed[:, s * rows : (s + 1) * rows, :].reshape(depth, half)
            part = dot(x[:, s * depth : (s + 1) * depth], basis, ((1,), (0,)))
            total = part if total is None else total + part
        proj.append(total.astype(BF16))
    width = out.shape[1] // 2
    stores = []
    for y in range(4):
        for zh in range(2):
            at = (y * 2 + zh) * 4 * width
            part = dot(g0[:, at : at + 4 * width], proj[0], ((0,), (0,))) + dot(
                g1[:, at : at + 4 * width], proj[1], ((0,), (0,))
            )
            part = (part * scale).astype(BF16)
            for x in range(4):
                sent[y * 4 + x, zh * width : (zh + 1) * width, :] = part[
                    x * width : (x + 1) * width
                ]
        own = pl.ds(4 * y, 4)
        stores.append(pltpu.make_async_copy(sent.at[own], out.at[own], sems.at[y]))
        stores[-1].start()
    for store in stores:
        store.wait()


def low_rank(x0, x1, g0, g1, mixed, scale):
    members, _, half = mixed.shape
    shape = (members, g0.shape[1] // members, half)
    return pl.pallas_call(
        functools.partial(low_kernel, scale),
        in_specs=[VMEM] * 5,
        out_specs=HBM,
        out_shape=jax.ShapeDtypeStruct(shape, BF16),
        scratch_shapes=[pltpu.VMEM(shape, BF16), pltpu.SemaphoreType.DMA((4,))],
        cost_estimate=pl.CostEstimate(flops=1 << 20, bytes_accessed=1 << 16, transcendentals=0),
        name="low_rank",
    )(x0, x1, g0, g1, mixed)


def line_kernel(came, out):
    total = came[0].astype(F32)
    for i in range(1, came.shape[0]):
        total = total + came[i].astype(F32)
    total = total.astype(BF16)
    cols = out.shape[1]
    for i in range(32):
        out[i] = total[(i // 8) * cols : (i // 8 + 1) * cols]


def to_line(came):
    _, rows, half = came.shape
    return pl.pallas_call(
        line_kernel,
        out_shape=jax.ShapeDtypeStruct((32, rows // 4, half), BF16),
        compiler_params=PARAMS,
        cost_estimate=pl.CostEstimate(flops=LINE_COST, bytes_accessed=1 << 16, transcendentals=0),
        name="to_line",
    )(came)


def total_kernel(parts, out):
    for c in range(2):
        total = None
        for zh in range(2):
            for i in range(8):
                part = parts[(zh * 2 + c) * 8 + i].astype(F32)
                total = part if total is None else total + part
        out[c] = total


def total_of(parts):
    return pl.pallas_call(
        total_kernel,
        out_shape=jax.ShapeDtypeStruct((2,) + parts.shape[1:], F32),
        compiler_params=PARAMS,
        cost_estimate=pl.CostEstimate(flops=COST, bytes_accessed=1 << 16, transcendentals=0),
        name="total",
    )(parts)


def feature_kernel(count, core, *refs):
    tokens, (weight, mixed), outs = refs[:count], refs[count : count + 2], refs[count + 2 : -3]
    rows, made, sems = refs[-3:]
    feat = weight.shape[0] // 2
    rows[:feat, :] = weight[pl.ds(pl.multiple_of(core[0] * feat, feat), feat), :]
    for g in range(16):
        group = mixed[:, 256 + g * 16 : 256 + (g + 1) * 16, :]
        rows[feat:, g * 128 : (g + 1) * 128] = group.reshape(feat, 128)
    stores = []
    for i in reversed(range(len(outs))):
        pair = jnp.concatenate([tokens[2 * i][...], tokens[2 * i + 1][...]], axis=0)
        made[i] = dot(pair, rows[...], ((1,), (1,))).astype(BF16)
        stores.append(pltpu.make_async_copy(made.at[i], outs[i], sems.at[i]))
        stores[-1].start()
    for store in stores:
        store.wait()


def features(core, tokens, weight, mixed):
    n = tokens[0].shape[0]
    count = len(tokens)
    shape = (2 * n, weight.shape[0])
    return pl.pallas_call(
        functools.partial(feature_kernel, count),
        in_specs=[pl.BlockSpec(memory_space=pltpu.SMEM)] + [VMEM] * (count + 2),
        out_specs=[HBM] * (count // 2),
        out_shape=[jax.ShapeDtypeStruct(shape, BF16)] * (count // 2),
        scratch_shapes=[
            pltpu.VMEM(weight.shape, BF16),
            pltpu.VMEM((count // 2,) + shape, BF16),
            pltpu.SemaphoreType.DMA((count // 2,)),
        ],
        cost_estimate=pl.CostEstimate(
            flops=FEATURE_COST, bytes_accessed=1 << 16, transcendentals=0
        ),
        name="features",
    )(core[None], *tokens, weight, mixed)


def assemble_kernel(where, near, up, down, down2, crossed, out):
    line, core = where[0], where[1]
    feat, n = near.shape[1] // 2, crossed.shape[1]
    for i, (ref, offset) in enumerate(((near, 0), (up, 1), (down, 7), (down2, 6))):
        for r in range(2):
            shard = lax.rem(line + offset + 4 * r, 8)
            at = pl.multiple_of((shard * 2 + core) * feat, feat)
            out[:, pl.ds(at, feat)] = ref[:n, r * feat : (r + 1) * feat]
            at = pl.multiple_of((shard * 2 + 1 - core) * feat, feat)
            out[:, pl.ds(at, feat)] = crossed[i, :, r * feat : (r + 1) * feat]


def assemble(where, pieces, crossed):
    _, n, wide = crossed.shape
    return pl.pallas_call(
        assemble_kernel,
        in_specs=[pl.BlockSpec(memory_space=pltpu.SMEM)] + [VMEM] * 5,
        out_shape=jax.ShapeDtypeStruct((n, 8 * wide), BF16),
        compiler_params=PARAMS,
        cost_estimate=pl.CostEstimate(flops=0, bytes_accessed=1 << 16, transcendentals=0),
        name="assemble",
    )(where, *pieces, crossed)


def ring(value, step):
    return lax.ppermute(value, RING, [(i, (i + step) % 16) for i in range(16)])


def swap_cores(value):
    return lax.ppermute(value, "c", [(0, 1), (1, 0)])


def on_device(inputs, out_grad, weight, proj_basis, first_moment, second_moment):
    core = lax.axis_index("c")
    line = lax.axis_index(LINE)
    plane = lax.axis_index(PLANE)
    n, feat = inputs.shape[0], weight.shape[0] // 2
    scale = 1.0 / math.sqrt(n * 512)
    half = proj_basis.shape[1] // 2

    rows = feat // 16
    piece = lax.dynamic_slice(weight, (core * feat + plane * rows, 0), (rows, weight.shape[1]))
    piece = ring(piece, 4)
    piece = piece.reshape(rows, 16, 128).transpose(1, 0, 2).reshape(16 * rows, 128)
    p_rows = proj_basis.shape[0] // 16
    p_piece = lax.dynamic_slice(proj_basis, (plane * p_rows, core * half), (p_rows, half))
    p_line = spread(p_piece, LINE, 8).reshape(8 * p_rows, half)

    grad_c = swap_cores(out_grad)
    inputs_c = swap_cores(inputs)
    after = ring(out_grad, -1)
    before = ring(out_grad, 1)
    p_line, after = lax.optimization_barrier((p_line, after))
    mixed = spread(jnp.concatenate([p_line, piece]), PLANE, 16)
    after2 = ring(after, -1)
    far = [before, swap_cores(before), after, swap_cores(after), after2, swap_cores(after2)]
    mixed, inputs_c, grad_c, far = lax.optimization_barrier((mixed, inputs_c, grad_c, far))

    low = low_rank(inputs, inputs_c, out_grad, grad_c, mixed, scale)
    low, mixed = lax.optimization_barrier((low, mixed))
    came = lax.all_to_all(low, PLANE, 0, 0, tiled=True)
    near, o_before, o_after, o_after2 = features(
        core, [out_grad, grad_c] + far, weight, mixed
    )
    line_parts = to_line(came)
    line_parts, o_after2 = lax.optimization_barrier((line_parts, o_after2))
    low = total_of(lax.all_to_all(line_parts, COLUMN, 0, 0, tiled=True))
    cols = out_grad.shape[1] // 64
    flat_grad = low.transpose(0, 2, 1).reshape(1, 2 * half * cols)
    new_first = beta_one * first_moment + (1.0 - beta_one) * flat_grad
    new_second = beta_two * second_moment + (1.0 - beta_two) * flat_grad * flat_grad
    corr_one = 1.0 - beta_one**STEP
    corr_two = 1.0 - beta_two**STEP
    direction = (new_first / corr_one / (jnp.sqrt(new_second / corr_two) + epsilon)).astype(BF16)
    direction = direction.reshape(2 * half, cols)
    update = jnp.dot(proj_basis, direction, preferred_element_type=F32)

    pieces = [near, ring(o_before, -1), ring(o_after, 1), ring(o_after2, 2)]
    crossed = swap_cores(jnp.stack([v[n:] for v in pieces]))
    input_grad = assemble(jnp.stack([line, core]), pieces, crossed)
    return (input_grad, new_first, new_second, update)


def solution(mesh):
    fine = Mesh(mesh.devices.reshape(SIZES), AXES)
    dp, fsdp = AXES[:4], AXES[4:]
    in_specs = (
        P(AXES, None),
        P(AXES, None),
        P(fsdp, None),
        P(fsdp, None),
        P(dp, None),
        P(dp, None),
    )
    out_specs = (P(AXES, None), P(dp, None), P(dp, None), P(fsdp, dp))
    return jax.shard_map(
        on_device, mesh=fine, in_specs=in_specs, out_specs=out_specs, check_vma=False
    )
```

```python
import functools
import math

import jax
import jax.numpy as jnp
from jax import lax
from jax.experimental import pallas as pl
from jax.experimental.pallas import tpu as pltpu
from jax.sharding import Mesh
from jax.sharding import PartitionSpec as P

STEP = 1000

beta_one = 0.9
beta_two = 0.999
epsilon = 1e-08

AXES = ("y", "zh", "x", "c", "q", "p")
SIZES = (4, 2, 4, 2, 4, 2)
PLANE = ("y", "x")
LINE = ("q", "p")
RING = ("zh", "q", "p")
COLUMN = ("zh", "c", "q", "p")
F32, BF16 = jnp.float32, jnp.bfloat16
COST = 20 << 30
LINE_COST = 20 << 30
FEATURE_COST = 1 << 20
HBM = pl.BlockSpec(memory_space=pltpu.HBM)
VMEM = pl.BlockSpec(memory_space=pltpu.VMEM)
PARAMS = pltpu.CompilerParams(vmem_limit_bytes=20 * 1024 * 1024)


def spread(block, axes, count):
    sent = jnp.broadcast_to(block[None], (count,) + block.shape)
    return lax.all_to_all(sent, axes, 0, 0, tiled=True)


def dot(a, b, dims):
    return lax.dot_general(a, b, (dims, ((), ())), preferred_element_type=F32)


def low_kernel(scale, x0, x1, g0, g1, mixed, out, xs, gs, basis, sent, sems):
    members, tail, half = basis.shape
    first = pltpu.make_async_copy(mixed.at[:, pl.ds(0, tail)], basis, sems.at[0])
    loads = [
        pltpu.make_async_copy(ref, buf, sems.at[1 + i])
        for i, (ref, buf) in enumerate(
            ((x0, xs.at[0]), (x1, xs.at[1]), (g0, gs.at[0]), (g1, gs.at[1]))
        )
    ]
    first.start()
    for load in loads:
        load.start()
    first.wait()
    rows = tail // 8
    depth = members * rows
    proj = []
    for i in range(2):
        loads[i].wait()
        total = None
        for s in range(8):
            part = dot(
                xs[i, :, s * depth : (s + 1) * depth],
                basis[:, s * rows : (s + 1) * rows, :].reshape(depth, half),
                ((1,), (0,)),
            )
            total = part if total is None else total + part
        proj.append(total.astype(BF16))
    loads[2].wait()
    loads[3].wait()
    width = out.shape[1] // 2
    stores = []
    for y in range(4):
        for zh in range(2):
            at = (y * 2 + zh) * 4 * width
            part = dot(gs[0, :, at : at + 4 * width], proj[0], ((0,), (0,))) + dot(
                gs[1, :, at : at + 4 * width], proj[1], ((0,), (0,))
            )
            part = (part * scale).astype(BF16)
            for x in range(4):
                sent[y * 4 + x, zh * width : (zh + 1) * width, :] = part[
                    x * width : (x + 1) * width
                ]
        own = pl.ds(4 * y, 4)
        stores.append(pltpu.make_async_copy(sent.at[own], out.at[own], sems.at[5 + y]))
        stores[-1].start()
    for store in stores:
        store.wait()


def low_rank(x0, x1, g0, g1, mixed, scale):
    members, _, half = mixed.shape
    shape = (members, g0.shape[1] // members, half)
    return pl.pallas_call(
        functools.partial(low_kernel, scale),
        in_specs=[HBM] * 5,
        out_specs=HBM,
        out_shape=jax.ShapeDtypeStruct(shape, BF16),
        scratch_shapes=[
            pltpu.VMEM((2,) + x0.shape, BF16),
            pltpu.VMEM((2,) + g0.shape, BF16),
            pltpu.VMEM((members, 256, half), BF16),
            pltpu.VMEM(shape, BF16),
            pltpu.SemaphoreType.DMA((9,)),
        ],
        cost_estimate=pl.CostEstimate(flops=1 << 20, bytes_accessed=1 << 16, transcendentals=0),
        name="low_rank",
    )(x0, x1, g0, g1, mixed)


def line_kernel(came, out):
    total = came[0].astype(F32)
    for i in range(1, came.shape[0]):
        total = total + came[i].astype(F32)
    total = total.astype(BF16)
    cols = out.shape[1]
    for i in range(32):
        out[i] = total[(i // 8) * cols : (i // 8 + 1) * cols]


def to_line(came):
    _, rows, half = came.shape
    return pl.pallas_call(
        line_kernel,
        out_shape=jax.ShapeDtypeStruct((32, rows // 4, half), BF16),
        compiler_params=PARAMS,
        cost_estimate=pl.CostEstimate(flops=LINE_COST, bytes_accessed=1 << 16, transcendentals=0),
        name="to_line",
    )(came)


def total_kernel(parts, out):
    for c in range(2):
        total = None
        for zh in range(2):
            for i in range(8):
                part = parts[(zh * 2 + c) * 8 + i].astype(F32)
                total = part if total is None else total + part
        out[c] = total


def total_of(parts):
    return pl.pallas_call(
        total_kernel,
        out_shape=jax.ShapeDtypeStruct((2,) + parts.shape[1:], F32),
        compiler_params=PARAMS,
        cost_estimate=pl.CostEstimate(flops=COST, bytes_accessed=1 << 16, transcendentals=0),
        name="total",
    )(parts)


def feature_kernel(count, core, *refs):
    tokens, (weight, mixed), outs = refs[:count], refs[count : count + 2], refs[count + 2 : -5]
    held, came, rows, made, sems = refs[-5:]
    feat = weight.shape[0] // 2
    other = pltpu.make_async_copy(mixed.at[:, pl.ds(256, 256)], came, sems.at[count])
    own = pltpu.make_async_copy(
        weight.at[pl.ds(pl.multiple_of(core[0] * feat, feat), feat)],
        rows.at[pl.ds(0, feat)],
        sems.at[count + 1],
    )
    loads = [pltpu.make_async_copy(ref, held.at[i], sems.at[i]) for i, ref in enumerate(tokens)]
    other.start()
    own.start()
    for load in reversed(loads):
        load.start()
    other.wait()
    for g in range(16):
        group = came[:, g * 16 : (g + 1) * 16, :]
        rows[feat:, g * 128 : (g + 1) * 128] = group.reshape(feat, 128)
    own.wait()
    stores = []
    for i in reversed(range(len(outs))):
        loads[2 * i + 1].wait()
        loads[2 * i].wait()
        pair = jnp.concatenate([held[2 * i], held[2 * i + 1]], axis=0)
        made[i] = dot(pair, rows[...], ((1,), (1,))).astype(BF16)
        stores.append(pltpu.make_async_copy(made.at[i], outs[i], sems.at[count + 2 + i]))
        stores[-1].start()
    for store in stores:
        store.wait()


def features(core, tokens, weight, mixed):
    n, depth = tokens[0].shape
    count = len(tokens)
    shape = (2 * n, weight.shape[0])
    return pl.pallas_call(
        functools.partial(feature_kernel, count),
        in_specs=[pl.BlockSpec(memory_space=pltpu.SMEM)] + [HBM] * (count + 2),
        out_specs=[HBM] * (count // 2),
        out_shape=[jax.ShapeDtypeStruct(shape, BF16)] * (count // 2),
        scratch_shapes=[
            pltpu.VMEM((count, n, depth), BF16),
            pltpu.VMEM((mixed.shape[0], 256, mixed.shape[2]), BF16),
            pltpu.VMEM(weight.shape, BF16),
            pltpu.VMEM((count // 2,) + shape, BF16),
            pltpu.SemaphoreType.DMA((count + 2 + count // 2,)),
        ],
        cost_estimate=pl.CostEstimate(
            flops=FEATURE_COST, bytes_accessed=1 << 16, transcendentals=0
        ),
        name="features",
    )(core[None], *tokens, weight, mixed)


def assemble_kernel(where, near, up, down, down2, crossed, out):
    line, core = where[0], where[1]
    feat, n = near.shape[1] // 2, crossed.shape[1]
    for i, (ref, offset) in enumerate(((near, 0), (up, 1), (down, 7), (down2, 6))):
        for r in range(2):
            shard = lax.rem(line + offset + 4 * r, 8)
            at = pl.multiple_of((shard * 2 + core) * feat, feat)
            out[:, pl.ds(at, feat)] = ref[:n, r * feat : (r + 1) * feat]
            at = pl.multiple_of((shard * 2 + 1 - core) * feat, feat)
            out[:, pl.ds(at, feat)] = crossed[i, :, r * feat : (r + 1) * feat]


def assemble(where, pieces, crossed):
    _, n, wide = crossed.shape
    return pl.pallas_call(
        assemble_kernel,
        in_specs=[pl.BlockSpec(memory_space=pltpu.SMEM)] + [VMEM] * 5,
        out_shape=jax.ShapeDtypeStruct((n, 8 * wide), BF16),
        compiler_params=PARAMS,
        cost_estimate=pl.CostEstimate(flops=0, bytes_accessed=1 << 16, transcendentals=0),
        name="assemble",
    )(where, *pieces, crossed)


def ring(value, step):
    return lax.ppermute(value, RING, [(i, (i + step) % 16) for i in range(16)])


def swap_cores(value):
    return lax.ppermute(value, "c", [(0, 1), (1, 0)])


def on_device(inputs, out_grad, weight, proj_basis, first_moment, second_moment):
    core = lax.axis_index("c")
    line = lax.axis_index(LINE)
    plane = lax.axis_index(PLANE)
    n, feat = inputs.shape[0], weight.shape[0] // 2
    scale = 1.0 / math.sqrt(n * 512)
    half = proj_basis.shape[1] // 2

    rows = feat // 16
    piece = lax.dynamic_slice(weight, (core * feat + plane * rows, 0), (rows, weight.shape[1]))
    piece = ring(piece, 4)
    piece = piece.reshape(rows, 16, 128).transpose(1, 0, 2).reshape(16 * rows, 128)
    p_rows = proj_basis.shape[0] // 16
    p_piece = lax.dynamic_slice(proj_basis, (plane * p_rows, core * half), (p_rows, half))
    p_line = spread(p_piece, LINE, 8).reshape(8 * p_rows, half)

    grad_c = swap_cores(out_grad)
    inputs_c = swap_cores(inputs)
    after = ring(out_grad, -1)
    before = ring(out_grad, 1)
    p_line, after = lax.optimization_barrier((p_line, after))
    mixed = spread(jnp.concatenate([p_line, piece]), PLANE, 16)
    after2 = ring(after, -1)
    far = [before, swap_cores(before), after, swap_cores(after), after2, swap_cores(after2)]
    mixed, inputs_c, grad_c, far = lax.optimization_barrier((mixed, inputs_c, grad_c, far))

    low = low_rank(inputs, inputs_c, out_grad, grad_c, mixed, scale)
    low, mixed = lax.optimization_barrier((low, mixed))
    came = lax.all_to_all(low, PLANE, 0, 0, tiled=True)
    near, o_before, o_after, o_after2 = features(
        core, [out_grad, grad_c] + far, weight, mixed
    )
    line_parts = to_line(came)
    line_parts, o_after2 = lax.optimization_barrier((line_parts, o_after2))
    low = total_of(lax.all_to_all(line_parts, COLUMN, 0, 0, tiled=True))
    cols = out_grad.shape[1] // 64
    flat_grad = low.transpose(0, 2, 1).reshape(1, 2 * half * cols)
    new_first = beta_one * first_moment + (1.0 - beta_one) * flat_grad
    new_second = beta_two * second_moment + (1.0 - beta_two) * flat_grad * flat_grad
    corr_one = 1.0 - beta_one**STEP
    corr_two = 1.0 - beta_two**STEP
    direction = (new_first / corr_one / (jnp.sqrt(new_second / corr_two) + epsilon)).astype(BF16)
    direction = direction.reshape(2 * half, cols)
    update = jnp.dot(proj_basis, direction, preferred_element_type=F32)

    pieces = [near, ring(o_before, -1), ring(o_after, 1), ring(o_after2, 2)]
    crossed = swap_cores(jnp.stack([v[n:] for v in pieces]))
    input_grad = assemble(jnp.stack([line, core]), pieces, crossed)
    return (input_grad, new_first, new_second, update)


def solution(mesh):
    fine = Mesh(mesh.devices.reshape(SIZES), AXES)
    dp, fsdp = AXES[:4], AXES[4:]
    in_specs = (
        P(AXES, None),
        P(AXES, None),
        P(fsdp, None),
        P(fsdp, None),
        P(dp, None),
        P(dp, None),
    )
    out_specs = (P(AXES, None), P(dp, None), P(dp, None), P(fsdp, dp))
    return jax.shard_map(
        on_device, mesh=fine, in_specs=in_specs, out_specs=out_specs, check_vma=False
    )
```

```python
import functools
import math

import jax
import jax.numpy as jnp
from jax import lax
from jax.experimental import pallas as pl
from jax.experimental.pallas import tpu as pltpu
from jax.sharding import Mesh
from jax.sharding import PartitionSpec as P

STEP = 1000

beta_one = 0.9
beta_two = 0.999
epsilon = 1e-08

AXES = ("y", "zh", "x", "c", "q", "p")
SIZES = (4, 2, 4, 2, 4, 2)
PLANE = ("y", "x")
LINE = ("q", "p")
RING = ("zh", "q", "p")
COLUMN = ("zh", "c", "q", "p")
F32, BF16 = jnp.float32, jnp.bfloat16
COST = 20 << 30
LINE_COST = 20 << 30
FEATURE_COST = 1 << 20
HBM = pl.BlockSpec(memory_space=pltpu.HBM)
VMEM = pl.BlockSpec(memory_space=pltpu.VMEM)
PARAMS = pltpu.CompilerParams(vmem_limit_bytes=20 * 1024 * 1024)


def spread(block, axes, count):
    sent = jnp.broadcast_to(block[None], (count,) + block.shape)
    return lax.all_to_all(sent, axes, 0, 0, tiled=True)


def dot(a, b, dims):
    return lax.dot_general(a, b, (dims, ((), ())), preferred_element_type=F32)


def low_kernel(scale, x0, x1, g0, g1, mixed, out, xs, gs, basis, sent, sems):
    members, tail, half = basis.shape
    first = pltpu.make_async_copy(mixed.at[:, pl.ds(0, tail)], basis, sems.at[0])
    loads = [
        pltpu.make_async_copy(ref, buf, sems.at[1 + i])
        for i, (ref, buf) in enumerate(
            ((x0, xs.at[0]), (x1, xs.at[1]), (g0, gs.at[0]), (g1, gs.at[1]))
        )
    ]
    first.start()
    for load in loads:
        load.start()
    first.wait()
    rows = tail // 8
    depth = members * rows
    proj = []
    for i in range(2):
        loads[i].wait()
        total = None
        for s in range(8):
            part = dot(
                xs[i, :, s * depth : (s + 1) * depth],
                basis[:, s * rows : (s + 1) * rows, :].reshape(depth, half),
                ((1,), (0,)),
            )
            total = part if total is None else total + part
        proj.append(total.astype(BF16))
    loads[2].wait()
    loads[3].wait()
    width = out.shape[1] // 2
    stores = []
    for y in range(4):
        for zh in range(2):
            at = (y * 2 + zh) * 4 * width
            part = dot(gs[0, :, at : at + 4 * width], proj[0], ((0,), (0,))) + dot(
                gs[1, :, at : at + 4 * width], proj[1], ((0,), (0,))
            )
            part = (part * scale).astype(BF16)
            for x in range(4):
                sent[y * 4 + x, zh * width : (zh + 1) * width, :] = part[
                    x * width : (x + 1) * width
                ]
        own = pl.ds(4 * y, 4)
        stores.append(pltpu.make_async_copy(sent.at[own], out.at[own], sems.at[5 + y]))
        stores[-1].start()
    for store in stores:
        store.wait()


def low_rank(x0, x1, g0, g1, mixed, scale):
    members, _, half = mixed.shape
    shape = (members, g0.shape[1] // members, half)
    return pl.pallas_call(
        functools.partial(low_kernel, scale),
        in_specs=[HBM] * 5,
        out_specs=HBM,
        out_shape=jax.ShapeDtypeStruct(shape, BF16),
        scratch_shapes=[
            pltpu.VMEM((2,) + x0.shape, BF16),
            pltpu.VMEM((2,) + g0.shape, BF16),
            pltpu.VMEM((members, 256, half), BF16),
            pltpu.VMEM(shape, BF16),
            pltpu.SemaphoreType.DMA((9,)),
        ],
        cost_estimate=pl.CostEstimate(flops=1 << 20, bytes_accessed=1 << 16, transcendentals=0),
        name="low_rank",
    )(x0, x1, g0, g1, mixed)


def line_kernel(came, out):
    total = came[0].astype(F32)
    for i in range(1, came.shape[0]):
        total = total + came[i].astype(F32)
    total = total.astype(BF16)
    cols = out.shape[1]
    for i in range(32):
        out[i] = total[(i // 8) * cols : (i // 8 + 1) * cols]


def to_line(came):
    _, rows, half = came.shape
    return pl.pallas_call(
        line_kernel,
        out_shape=jax.ShapeDtypeStruct((32, rows // 4, half), BF16),
        compiler_params=PARAMS,
        cost_estimate=pl.CostEstimate(flops=LINE_COST, bytes_accessed=1 << 16, transcendentals=0),
        name="to_line",
    )(came)


def total_kernel(parts, out):
    for c in range(2):
        total = None
        for zh in range(2):
            for i in range(8):
                part = parts[(zh * 2 + c) * 8 + i].astype(F32)
                total = part if total is None else total + part
        out[c] = total


def total_of(parts):
    return pl.pallas_call(
        total_kernel,
        out_shape=jax.ShapeDtypeStruct((2,) + parts.shape[1:], F32),
        compiler_params=PARAMS,
        cost_estimate=pl.CostEstimate(flops=COST, bytes_accessed=1 << 16, transcendentals=0),
        name="total",
    )(parts)


def feature_kernel(count, core, *refs):
    tokens, (weight, mixed), outs = refs[:count], refs[count : count + 2], refs[count + 2 : -5]
    held, came, rows, made, sems = refs[-5:]
    feat = weight.shape[0] // 2
    other = pltpu.make_async_copy(mixed.at[:, pl.ds(256, 256)], came, sems.at[count])
    own = pltpu.make_async_copy(
        weight.at[pl.ds(pl.multiple_of(core[0] * feat, feat), feat)],
        rows.at[pl.ds(0, feat)],
        sems.at[count + 1],
    )
    loads = [pltpu.make_async_copy(ref, held.at[i], sems.at[i]) for i, ref in enumerate(tokens)]
    other.start()
    own.start()
    for load in reversed(loads):
        load.start()
    other.wait()
    for g in range(16):
        group = came[:, g * 16 : (g + 1) * 16, :]
        rows[feat:, g * 128 : (g + 1) * 128] = group.reshape(feat, 128)
    own.wait()
    stores = []
    for i in reversed(range(len(outs))):
        loads[2 * i + 1].wait()
        loads[2 * i].wait()
        pair = jnp.concatenate([held[2 * i], held[2 * i + 1]], axis=0)
        made[i] = dot(pair, rows[...], ((1,), (1,))).astype(BF16)
        stores.append(pltpu.make_async_copy(made.at[i], outs[i], sems.at[count + 2 + i]))
        stores[-1].start()
    for store in stores:
        store.wait()


def features(core, tokens, weight, mixed):
    n, depth = tokens[0].shape
    count = len(tokens)
    shape = (2 * n, weight.shape[0])
    return pl.pallas_call(
        functools.partial(feature_kernel, count),
        in_specs=[pl.BlockSpec(memory_space=pltpu.SMEM)] + [HBM] * (count + 2),
        out_specs=[HBM] * (count // 2),
        out_shape=[jax.ShapeDtypeStruct(shape, BF16)] * (count // 2),
        scratch_shapes=[
            pltpu.VMEM((count, n, depth), BF16),
            pltpu.VMEM((mixed.shape[0], 256, mixed.shape[2]), BF16),
            pltpu.VMEM(weight.shape, BF16),
            pltpu.VMEM((count // 2,) + shape, BF16),
            pltpu.SemaphoreType.DMA((count + 2 + count // 2,)),
        ],
        cost_estimate=pl.CostEstimate(
            flops=FEATURE_COST, bytes_accessed=1 << 16, transcendentals=0
        ),
        name="features",
    )(core[None], *tokens, weight, mixed)


def assemble_kernel(where, near, up, down, down2, crossed, out):
    line, core = where[0], where[1]
    feat, n = near.shape[1] // 2, crossed.shape[1]
    for i, (ref, offset) in enumerate(((near, 0), (up, 1), (down, 7), (down2, 6))):
        for r in range(2):
            shard = lax.rem(line + offset + 4 * r, 8)
            at = pl.multiple_of((shard * 2 + core) * feat, feat)
            out[:, pl.ds(at, feat)] = ref[:n, r * feat : (r + 1) * feat]
            at = pl.multiple_of((shard * 2 + 1 - core) * feat, feat)
            out[:, pl.ds(at, feat)] = crossed[i, :, r * feat : (r + 1) * feat]


def assemble(where, pieces, crossed):
    _, n, wide = crossed.shape
    return pl.pallas_call(
        assemble_kernel,
        in_specs=[pl.BlockSpec(memory_space=pltpu.SMEM)] + [VMEM] * 5,
        out_shape=jax.ShapeDtypeStruct((n, 8 * wide), BF16),
        compiler_params=PARAMS,
        cost_estimate=pl.CostEstimate(flops=0, bytes_accessed=1 << 16, transcendentals=0),
        name="assemble",
    )(where, *pieces, crossed)


def ring(value, step):
    return lax.ppermute(value, RING, [(i, (i + step) % 16) for i in range(16)])


def swap_cores(value):
    return lax.ppermute(value, "c", [(0, 1), (1, 0)])


def on_device(inputs, out_grad, weight, proj_basis, first_moment, second_moment):
    core = lax.axis_index("c")
    line = lax.axis_index(LINE)
    plane = lax.axis_index(PLANE)
    n, feat = inputs.shape[0], weight.shape[0] // 2
    scale = 1.0 / math.sqrt(n * 512)
    half = proj_basis.shape[1] // 2

    rows = feat // 16
    piece = lax.dynamic_slice(weight, (core * feat + plane * rows, 0), (rows, weight.shape[1]))
    piece = ring(piece, 4)
    piece = piece.reshape(rows, 16, 128).transpose(1, 0, 2).reshape(16 * rows, 128)
    p_rows = proj_basis.shape[0] // 16
    p_piece = lax.dynamic_slice(proj_basis, (plane * p_rows, core * half), (p_rows, half))
    p_line = spread(p_piece, LINE, 8).reshape(8 * p_rows, half)

    grad_c = swap_cores(out_grad)
    inputs_c = swap_cores(inputs)
    after = ring(out_grad, -1)
    before = ring(out_grad, 1)
    p_line, after = lax.optimization_barrier((p_line, after))
    mixed = spread(jnp.concatenate([p_line, piece]), PLANE, 16)
    after2 = ring(after, -1)
    far = [before, swap_cores(before), after, swap_cores(after), after2, swap_cores(after2)]
    mixed, inputs_c, grad_c, far = lax.optimization_barrier((mixed, inputs_c, grad_c, far))

    low = low_rank(inputs, inputs_c, out_grad, grad_c, mixed, scale)
    low, mixed = lax.optimization_barrier((low, mixed))
    came = lax.all_to_all(low, PLANE, 0, 0, tiled=True)
    near, o_before, o_after, o_after2 = features(
        core, [out_grad, grad_c] + far, weight, mixed
    )
    line_parts = to_line(came)
    low = total_of(lax.all_to_all(line_parts, COLUMN, 0, 0, tiled=True))
    cols = out_grad.shape[1] // 64
    pieces = [near, ring(o_before, -1), ring(o_after, 1), ring(o_after2, 2)]
    crossed = swap_cores(jnp.stack([v[n:] for v in pieces]))
    crossed, low = lax.optimization_barrier((crossed, low))
    flat_grad = low.transpose(0, 2, 1).reshape(1, 2 * half * cols)
    new_first = beta_one * first_moment + (1.0 - beta_one) * flat_grad
    new_second = beta_two * second_moment + (1.0 - beta_two) * flat_grad * flat_grad
    corr_one = 1.0 - beta_one**STEP
    corr_two = 1.0 - beta_two**STEP
    direction = (new_first / corr_one / (jnp.sqrt(new_second / corr_two) + epsilon)).astype(BF16)
    direction = direction.reshape(2 * half, cols)
    update = jnp.dot(proj_basis, direction, preferred_element_type=F32)

    input_grad = assemble(jnp.stack([line, core]), pieces, crossed)
    return (input_grad, new_first, new_second, update)


def solution(mesh):
    fine = Mesh(mesh.devices.reshape(SIZES), AXES)
    dp, fsdp = AXES[:4], AXES[4:]
    in_specs = (
        P(AXES, None),
        P(AXES, None),
        P(fsdp, None),
        P(fsdp, None),
        P(dp, None),
        P(dp, None),
    )
    out_specs = (P(AXES, None), P(dp, None), P(dp, None), P(fsdp, dp))
    return jax.shard_map(
        on_device, mesh=fine, in_specs=in_specs, out_specs=out_specs, check_vma=False
    )
```
